32 devices in a mesh: band: 4 (over y, core), order: 8 (over z, x).
Axes of the slice: x: 2, y: 2, z: 4, core: 2. Of those that a mesh axis runs over, the one named last changes fastest.
Arguments:
- thickness: float32 [524288], P(('band', 'order')), may hold values from -24 to 24
- tile_weights: float32 [4096, 128, 128], P(('band', 'order')), may hold values from -0.5 to 0.5
- tile_dest: int32 [4096, 1], P(('band', 'order')), may hold values from 0 to 31; in each aligned block of 128 rows (0 to 127, 128 to 255, ...) at most 8 rows name the same one
- tile_row: int32 [4096], P(('band', 'order')), may hold values from 0 to 127
- tile_col: int32 [4096], P(('band', 'order')), may hold values from 0 to 63
- window: int32 [8], replicated, may hold values from 0 to 4095, as said below
- quad_weights: float32 [4096], P('band'), may hold values from 0.5 to 2
- legendre: float32 [8, 4096, 4096], P('order', 'band'), may hold values from -0.09375 to 0.09375
- love_code: int32 [4096], replicated, may hold values from 100 to 2000
Outputs:
- uplift: float32 [524288], P(('band', 'order'))
- coefficients: float32 [8, 2, 4096], P('order')
The draws below stay inside these ranges and needn't reach their ends.
Inputs may be any that keep to these rules, and one draw needn't show every extreme that they name: `window`: the orders are distinct and below 4096; both 0 and 4095 are among them. `tile_dest`: among the tiles of one device, at most 8 have the same owner.
All inputs are finite; a program needn't handle non-finite values.
Results may differ from the reference program's by a relative error of at most 0.000098.
Values sent between devices are 32-bit elements; how exact they have to be, the bound alone decides.
No kernel may reach another device: no remote copies, remote signals or barrier semaphores. Data moves between devices by JAX's collectives and lax.ppermute only.
A program may use at most 64 MiB of HBM per device.

```python
import math
import jax
import jax.numpy as jnp
import numpy as np
from jax import lax

NLAT = 4096
NLON = 8192
LDEG = 4096
TILES_DEV = 128
ORDERS = 8
TILES = 4096
ELEMS = 524288
LAT_DEV = 128
CAP = 8
DEVICES = 32


def draw_window(key, part):
    half = NLON // 2
    inner = 1 + jax.random.permutation(jax.random.fold_in(key, 11), half - 2)[:ORDERS - 2]
    picked = jnp.concatenate([jnp.array([0, half - 1], jnp.int32), inner.astype(jnp.int32)])
    shuffle = jax.random.permutation(jax.random.fold_in(key, 12), ORDERS)
    return picked[shuffle]


def place_ends(entries, stream_key, smallest, top_value):
    longest = entries.shape.index(max(entries.shape))
    spots = []
    for shift in (0, 1):
        where = [jax.random.randint(jax.random.fold_in(stream_key, axis), (), 0, length) for axis, length in enumerate(entries.shape)]
        where[longest] = (where[longest] + shift) % entries.shape[longest]
        spots.append(tuple(where))
    return entries.at[spots[0]].set(smallest).at[spots[1]].set(top_value)


def block_levels(rng, extent, shards, smallest, largest):
    def one(position, shards_of):
        heights = jax.random.uniform(jax.random.fold_in(jax.random.fold_in(rng, 6), position), (shards_of,), jnp.float32, smallest / len(shards), largest / len(shards))
        return jnp.repeat(jnp.exp(heights), extent[position] // shards_of).reshape((-1,) + (1,) * (len(extent) - position - 1))

    level = one(*shards[0])
    for cut in shards[1:]:
        level = level * one(*cut)
    return level


def shared_out(stream_key, own, number, rows, number_of, top, limit, lean):
    order = jax.random.permutation(stream_key, number_of)
    crowded, common = shares(number_of, rows * top, limit, lean, True), shares(number_of, rows * top, limit, lean, False)
    places = jnp.arange(number_of)

    def named(sizes, rotation):
        used = int((sizes > 0).sum())
        fixed = max(1, used // 4)
        passed = fixed + (places - fixed + rotation * (used - fixed)) % max(1, number_of - fixed)
        return jnp.zeros((number_of,), jnp.int32).at[order[jnp.where(places < fixed, places, passed)]].set(jnp.asarray(sizes, jnp.int32))

    sizes = jnp.where(number % 4 == 0, named(crowded, number // 4), named(common, number - number // 4 - 1))
    mixed = jax.random.permutation(jax.random.fold_in(own, 3), number_of)
    source_of, taker = mixed[0:number_of // 2 * 2:2], mixed[1:number_of // 2 * 2:2]
    slack = jnp.minimum(sizes[source_of] - 1, limit - sizes[taker]) // 2
    slack = jnp.where((source_of == order[0]) | (taker == order[0]) | (sizes[taker] == 0), 0, jnp.maximum(slack, 0))
    passed = jax.random.randint(jax.random.fold_in(own, 4), (number_of // 2,), 0, 1 << 20) % (slack + 1)
    sizes = sizes.at[source_of].add(-passed).at[taker].add(passed)
    labels = jnp.searchsorted(jnp.cumsum(sizes), jnp.arange(rows * top), side="right").astype(jnp.int32)
    table = labels.reshape(top, rows).T
    table = table[jax.random.permutation(jax.random.fold_in(own, 1), rows)]
    rotation = jax.random.randint(jax.random.fold_in(own, 2), (rows, 1), 0, top)
    return jnp.take_along_axis(table, (jnp.arange(top)[None, :] + rotation) % top, axis=1)


def shares(count, total, most, lean, full):
    weights = [(1 << 20) // math.isqrt(rank ** lean) + 1 for rank in range(1, count + 1)]
    largest = most if full else min(most, max(-(-total // count), total * weights[0] // sum(weights)))
    least = 1 if total - largest >= count - 1 else 0
    given, rest = [largest] + [least] * (count - 1), total - largest - least * (count - 1)
    while rest > 0:
        candidates = [i for i in range(1, count) if given[i] < largest] or [i for i in range(1, count) if given[i] < most]
        whole, left = sum([weights[i] for i in candidates]), rest
        for i in candidates:
            extra = min(most - given[i], max(1, left * weights[i] // whole), rest)
            given[i] = given[i] + extra
            rest = rest - extra
    return np.array(given)


def noise(stream_key, extent, scale, limit, cuts=(), held_as=jnp.bfloat16):
    values = scale * jax.random.normal(stream_key, extent, jnp.float32)
    if cuts:
        values = values * block_levels(stream_key, extent, cuts, -0.22, 0.18)
    return jnp.clip(values, -limit, limit).astype(held_as)


def setup_inputs(seed: int = 0) -> dict:
    key_list = jax.random.split(jax.random.key(seed), 10)
    thickness = noise(key_list[0], (ELEMS,), 4.0, 24.0, ((0, 32),), jnp.float32)
    tile_weights = noise(key_list[1], (TILES, 128, 128), 128 ** -0.5, 0.5, ((0, 32),), jnp.float32)
    tile_dest_keys = jax.random.split(jax.random.fold_in(key_list[2], 1), TILES // TILES_DEV)
    tile_dest_turns = jax.random.permutation(jax.random.fold_in(key_list[2], 3), TILES // TILES_DEV)
    tile_dest = jax.vmap(lambda own, number: shared_out(jax.random.fold_in(key_list[2], 2), own, number, TILES_DEV, DEVICES, 1, CAP, 2))(tile_dest_keys, tile_dest_turns).reshape((TILES, 1))
    tile_row = place_ends(jax.random.randint(key_list[3], (TILES,), 0, LAT_DEV), jax.random.fold_in(key_list[3], 1), 0, LAT_DEV - 1).astype(jnp.int32)
    tile_col = place_ends(jax.random.randint(key_list[4], (TILES,), 0, NLON // 128), jax.random.fold_in(key_list[4], 1), 0, (NLON // 128) - 1).astype(jnp.int32)
    window = draw_window(jax.random.fold_in(key_list[9], 71), 0)
    quad_weights = jnp.clip(jnp.exp(math.log(2.0) - 1.3862944 * jax.random.uniform(key_list[6], (NLAT,), jnp.float32) ** block_levels(key_list[6], (NLAT,), ((0, 4),), -0.2, 0.2)), 0.5, 2.0)
    legendre = noise(key_list[7], (ORDERS, NLAT, LDEG), NLAT ** -0.5, 0.09375, ((0, 8), (1, 4)), jnp.float32)
    love_code = place_ends(jax.random.randint(key_list[8], (LDEG,), 100, 2001), jax.random.fold_in(key_list[8], 1), 100, 2000).astype(jnp.int32)
    return dict(thickness=thickness, tile_weights=tile_weights, tile_dest=tile_dest, tile_row=tile_row, tile_col=tile_col, window=window, quad_weights=quad_weights, legendre=legendre, love_code=love_code)


def make_table(window, count):
    column = jnp.arange(count, dtype=jnp.int32)
    phase = (column[:, None] * window[None, :].astype(jnp.int32)) % count
    angle = phase.astype(jnp.float32) * (2.0 * math.pi / count)
    return jnp.concatenate([jnp.cos(angle), jnp.sin(angle)], axis=1)


def reference(thickness, tile_weights, tile_dest, tile_row, tile_col, window, quad_weights, legendre, love_code):
    upper_limit = lax.Precision.HIGHEST
    blocks_per_row = NLON // 128
    elements = thickness.reshape(TILES, 128)
    cells = jnp.einsum("tce,te->tc", tile_weights, elements, precision=upper_limit)
    target = (tile_dest[:, 0] * LAT_DEV + tile_row) * blocks_per_row + tile_col
    grid = jnp.zeros((NLAT * blocks_per_row, 128), jnp.float32).at[target].add(cells)
    grid = grid.reshape(NLAT, NLON)
    table = make_table(window, NLON)
    spectra = jnp.dot(grid, table, precision=upper_limit) * (NLON ** -0.5)
    weight_applied = (spectra * quad_weights[:, None]).reshape(NLAT, 2, ORDERS)
    love = love_code.astype(jnp.float32) / 1000.0
    running_sum = jnp.einsum("qek,kqd->ked", weight_applied, legendre, precision=upper_limit)
    coefficients = running_sum * love[None, None, :]
    field_arrays = jnp.einsum("shq,saq->has", legendre, coefficients, precision=upper_limit)
    field_arrays = field_arrays.reshape(NLAT, 2 * ORDERS)
    response = jnp.dot(field_arrays, table.T, precision=upper_limit) * ((2 * ORDERS) ** -0.5)
    picked = response.reshape(NLAT * blocks_per_row, 128)[target]
    uplift = jnp.einsum("tce,tc->te", tile_weights, picked, precision=upper_limit).reshape(ELEMS)
    return uplift, coefficients
```

```python
import functools
import math

import jax
import jax.numpy as jnp
from jax import lax
from jax.experimental import pallas as pl
from jax.experimental.pallas import tpu as pltpu
from jax.sharding import PartitionSpec as P

NLON = 8192
LANES = 128
BLOCKS = NLON // LANES
CHUNK = 16
F32 = jnp.float32
BF16 = jnp.bfloat16
MIB = 1 << 20
EARLY = 3


def split(x, parts):
    out = []
    for _ in range(parts):
        piece = x.astype(BF16)
        out.append(piece)
        x = x - piece.astype(F32)
    return out


def trig(phase, period):
    angle = phase.astype(F32) * (2.0 * math.pi / period)
    return jnp.cos(angle), jnp.sin(angle)


def project_kernel(
    bands,
    order_count,
    lat_band,
    window_hbm,
    thickness_hbm,
    dest_hbm,
    row_hbm,
    col_hbm,
    weights,
    legendre,
    basis,
    rot,
    outgoing,
    early,
    held,
    window,
    thickness,
    dest,
    row,
    col,
    sems,
):
    tiles = held.shape[0]
    orders = window.shape[0]
    copies = [
        pltpu.make_async_copy(
            weights.at[pl.ds(c * CHUNK, CHUNK)], held.at[pl.ds(c * CHUNK, CHUNK)], sems.at[c]
        )
        for c in range(tiles // CHUNK)
    ]
    small = [
        pltpu.make_async_copy(src, dst, sems.at[tiles // CHUNK + i])
        for i, (src, dst) in enumerate(
            (
                (window_hbm, window),
                (col_hbm, col),
                (thickness_hbm, thickness),
                (dest_hbm, dest),
                (row_hbm, row),
            )
        )
    ]
    ahead = pltpu.make_async_copy(
        legendre.at[pl.ds(0, early.shape[0])], early, sems.at[tiles // CHUNK + 5]
    )
    for copy in small + copies + [ahead]:
        copy.start()
    for copy in small:
        copy.wait()
    sub = lax.broadcasted_iota(jnp.int32, (orders, LANES), 0)
    lane = lax.broadcasted_iota(jnp.int32, (orders, LANES), 1)
    order = jnp.zeros((orders, LANES), jnp.int32)
    for m in range(orders):
        order = jnp.where(sub == m, window[m], order)
    cos_in, sin_in = trig((order * lane) & (NLON - 1), NLON)
    cos_block, sin_block = trig((order * col[...]) & (BLOCKS - 1), BLOCKS)
    rot[:orders] = cos_block
    rot[orders:] = sin_block
    inner = jnp.concatenate([cos_in, sin_in], axis=0)
    high, low = split(inner, 2)
    left = jnp.concatenate([high, low], axis=0)
    left = jnp.concatenate([left, left], axis=1)
    wide_lane = lax.broadcasted_iota(jnp.int32, (2 * orders, LANES), 1)
    sums = jnp.zeros((2 * orders, tiles), F32)
    for c in range(tiles // CHUNK):
        copies[c].wait()
        pieces = []
        for i in range(CHUNK):
            high, low = split(held[c * CHUNK + i], 2)
            pieces.append(jnp.concatenate([high, low], axis=0))
        product = jnp.dot(left, jnp.concatenate(pieces, axis=1), preferred_element_type=F32)
        product = product[: 2 * orders] + product[2 * orders :]
        for i in range(CHUNK):
            t = c * CHUNK + i
            mine = product[:, i * LANES : (i + 1) * LANES]
            basis[t] = mine
            total = jnp.sum(mine * thickness[t : t + 1, :], axis=1, keepdims=True)
            sums = jnp.where(wide_lane == t, total, sums)
    by_cos, by_sin = sums[:orders], sums[orders:]
    scale = NLON**-0.5
    cos_part = (by_cos * cos_block - by_sin * sin_block) * scale
    sin_part = (by_cos * sin_block + by_sin * cos_block) * scale
    latitude = dest[...] * (lat_band // order_count) + row[...]
    for b in range(bands):
        place = (latitude - b * lat_band).astype(F32)
        for o in range(order_count):
            d = b * order_count + o
            outgoing[d, :, 0:LANES] = cos_part[o : o + 1]
            outgoing[d, :, LANES : 2 * LANES] = sin_part[o : o + 1]
            outgoing[d, :, 2 * LANES : 3 * LANES] = place
    ahead.wait()


def places(arrived, s):
    latitude = arrived[s, :, 2 * LANES : 3 * LANES].astype(jnp.int32)
    return latitude >> 7, latitude & (LANES - 1)


def selector(arrived, s):
    sub = lax.broadcasted_iota(jnp.int32, (LANES, LANES), 0)
    _, low = places(arrived, s)
    return jnp.where(sub == low, 1.0, 0.0).astype(BF16)


def analyse_kernel(
    arrived, quad_hbm, legendre, early, partial, late, spread, quad, total, sem, sems
):
    begun = early.shape[0] // LANES
    copies = [
        pltpu.make_async_copy(
            legendre.at[pl.ds((begun + i) * LANES, LANES)],
            late.at[pl.ds(i * LANES, LANES)],
            sems.at[i],
        )
        for i in range(late.shape[0] // LANES)
    ]
    fetch = pltpu.make_async_copy(quad_hbm, quad, sem)
    for copy in [fetch] + copies:
        copy.start()
    devices = arrived.shape[0]
    groups = quad.shape[0]
    rows = 2 * groups
    sub = lax.broadcasted_iota(jnp.int32, (rows, LANES), 0)
    group = jnp.where(sub >= groups, sub - groups, sub)
    select, value = [], []
    for s in range(devices):
        high, _ = places(arrived, s)
        both = jnp.where(
            sub < groups, arrived[s, :, 0:LANES], arrived[s, :, LANES : 2 * LANES]
        )
        value.append(jnp.where(group == high, both, 0.0))
        select.append(selector(arrived, s))
    select = jnp.concatenate(select, axis=1)
    value = jnp.concatenate(value, axis=1)
    spectra = jnp.zeros((LANES, rows), F32)
    for piece in reversed(split(value, 3)):
        spectra = spectra + lax.dot_general(
            select, piece, (((1,), (1,)), ((), ())), preferred_element_type=F32
        )
    fetch.wait()
    weight = quad[...]
    weight = jnp.concatenate([weight, weight], axis=0)
    weight = jnp.concatenate([weight, jnp.zeros((LANES - rows, LANES), F32)], axis=0)
    spectra = spectra * jnp.transpose(weight)[:, :rows]
    for e in range(2):
        for h in range(groups):
            k = e * groups + h
            spread[e, h * LANES : (h + 1) * LANES, :] = jnp.broadcast_to(
                spectra[:, k : k + 1], (LANES, LANES)
            )
    wide = 8
    degrees = legendre.shape[1]
    for h in range(groups):
        table, base = (early, h) if h < begun else (late, h - begun)
        if h >= begun:
            copies[h - begun].wait()

        def body(n, carry):
            start = pl.multiple_of(n * (wide * LANES), wide * LANES)
            sums = [jnp.zeros((8, LANES), F32)] * (2 * wide)
            for j in range(LANES // 8):
                at = slice(h * LANES + j * 8, h * LANES + j * 8 + 8)
                row = slice(base * LANES + j * 8, base * LANES + j * 8 + 8)
                first, second = spread[0, at, :], spread[1, at, :]
                for k in range(wide):
                    p = table[row, pl.ds(start + k * LANES, LANES)]
                    sums[2 * k] = sums[2 * k] + p * first
                    sums[2 * k + 1] = sums[2 * k + 1] + p * second
            for k in range(wide):
                cut = pl.ds(start + k * LANES, LANES)
                for e in range(2):
                    got = sums[2 * k + e]
                    if h > 0:
                        got = got + total[e, :, cut]
                    if h < groups - 1:
                        total[e, :, cut] = got
                    else:
                        partial[e : e + 1, cut] = jnp.sum(got, axis=0, keepdims=True)
            return carry

        lax.fori_loop(0, degrees // (wide * LANES), body, 0)


def synthesise_kernel(
    share_0, share_1, share_2, share_3, love, arrived, early, late, coefficients, reply, spread, fields
):
    devices = arrived.shape[0]
    degrees = early.shape[1]
    begun = early.shape[0] // LANES
    groups = begun + late.shape[0] // LANES
    rows = 2 * groups
    total = (share_0[...] + share_1[...]) + (share_2[...] + share_3[...])
    scaled = total * (love[...].astype(F32) / 1000.0)
    coefficients[...] = scaled
    for e in range(2):
        spread[e] = jnp.broadcast_to(scaled[e : e + 1], (8, degrees))
    lane = lax.broadcasted_iota(jnp.int32, (8, LANES), 1)
    fields[...] = jnp.zeros_like(fields)

    def body(table, base, h, carry):
        for half in range(2):
            sums = [jnp.zeros((8, LANES), F32)] * 16
            for k in range(degrees // LANES):
                cut = slice(k * LANES, (k + 1) * LANES)
                first, second = spread[0, :, cut], spread[1, :, cut]
                for i in range(8):
                    at = pl.ds(pl.multiple_of((h - base) * LANES, LANES) + (half * 8 + i) * 8, 8)
                    p = table[at, cut]
                    sums[2 * i] = sums[2 * i] + p * first
                    sums[2 * i + 1] = sums[2 * i + 1] + p * second
            for i in range(8):
                g = half * 8 + i
                first = jnp.sum(sums[2 * i], axis=1, keepdims=True)
                second = jnp.sum(sums[2 * i + 1], axis=1, keepdims=True)
                old = fields[g * 8 : (g + 1) * 8, :]
                old = jnp.where(lane == h, first, old)
                fields[g * 8 : (g + 1) * 8, :] = jnp.where(lane == h + groups, second, old)
        return carry

    lax.fori_loop(0, begun, functools.partial(body, early, 0), 0)
    lax.fori_loop(begun, groups, functools.partial(body, late, begun), 0)
    turned = jnp.transpose(fields[...])[:rows]
    select = jnp.concatenate([selector(arrived, s) for s in range(devices)], axis=1)
    found = jnp.zeros((rows, devices * LANES), F32)
    for piece in reversed(split(turned, 3)):
        found = found + jnp.dot(piece, select, preferred_element_type=F32)
    sub = lax.broadcasted_iota(jnp.int32, (rows, LANES), 0)
    group = jnp.where(sub >= groups, sub - groups, sub)
    for s in range(devices):
        high, _ = places(arrived, s)
        here = jnp.where(group == high, found[:, s * LANES : (s + 1) * LANES], 0.0)
        reply[s, :, 0:LANES] = jnp.sum(here[:groups], axis=0, keepdims=True)
        reply[s, :, LANES : 2 * LANES] = jnp.sum(here[groups:], axis=0, keepdims=True)


def return_kernel(bands, answer, rot, basis, uplift, at_tile):
    tiles = basis.shape[0]
    orders = rot.shape[0] // 2
    order_count = answer.shape[0] // bands
    for e in range(2):
        for o in range(order_count):
            got = answer[o, :, e * LANES : (e + 1) * LANES]
            for b in range(1, bands):
                got = got + answer[b * order_count + o, :, e * LANES : (e + 1) * LANES]
            at_tile[e * orders + o : e * orders + o + 1, :] = got
    by_cos, by_sin = at_tile[:orders], at_tile[orders:]
    cos_block, sin_block = rot[:orders], rot[orders:]
    scale = (2 * orders) ** -0.5
    turned = jnp.concatenate(
        [
            (by_cos * cos_block + by_sin * sin_block) * scale,
            (by_sin * cos_block - by_cos * sin_block) * scale,
        ],
        axis=0,
    )
    for t in range(tiles):
        uplift[t : t + 1, :] = jnp.sum(basis[t] * turned[:, t : t + 1], axis=0, keepdims=True)


def in_hbm(x):
    return pltpu.with_memory_space_constraint(x, pltpu.HBM)


VMEM = pl.BlockSpec(memory_space=pltpu.VMEM)
ANY = pl.BlockSpec(memory_space=pl.ANY)


def on_device(
    bands,
    order_count,
    thickness,
    tile_weights,
    tile_dest,
    tile_row,
    tile_col,
    window,
    quad_weights,
    legendre,
    love_code,
):
    devices = bands * order_count
    axes = ("band", "order")
    tiles = tile_weights.shape[0]
    lat_band = quad_weights.shape[0]
    orders = window.shape[0]
    degrees = legendre.shape[2]
    assert tiles == LANES and legendre.shape[0] == 1 and orders == order_count
    assert lat_band % LANES == 0 and degrees % (8 * LANES) == 0 and tiles % CHUNK == 0
    legendre = in_hbm(legendre.reshape(lat_band, degrees))
    groups = lat_band // LANES
    first = max(1, groups * EARLY // 8) * LANES

    basis, rot, outgoing, early = pl.pallas_call(
        functools.partial(project_kernel, bands, order_count, lat_band),
        out_shape=(
            jax.ShapeDtypeStruct((tiles, 2 * orders, LANES), F32),
            jax.ShapeDtypeStruct((2 * orders, tiles), F32),
            jax.ShapeDtypeStruct((devices, 1, 3 * LANES), F32),
            pltpu.VMEM((first, degrees), F32),
        ),
        in_specs=[ANY] * 7,
        out_specs=(VMEM,) * 4,
        scratch_shapes=[
            pltpu.VMEM((tiles, LANES, LANES), F32),
            pltpu.SMEM((orders,), jnp.int32),
            pltpu.VMEM((tiles, LANES), F32),
            pltpu.VMEM((1, tiles), jnp.int32),
            pltpu.VMEM((1, tiles), jnp.int32),
            pltpu.VMEM((1, tiles), jnp.int32),
            pltpu.SemaphoreType.DMA((tiles // CHUNK + 6,)),
        ],
        cost_estimate=pl.CostEstimate(
            flops=0, transcendentals=0, bytes_accessed=10 * MIB
        ),
        compiler_params=pltpu.CompilerParams(vmem_limit_bytes=20 * MIB),
        name="project",
    )(
        in_hbm(window),
        in_hbm(thickness.reshape(tiles, LANES)),
        in_hbm(tile_dest.reshape(1, tiles)),
        in_hbm(tile_row.reshape(1, tiles)),
        in_hbm(tile_col.reshape(1, tiles)),
        in_hbm(tile_weights),
        legendre,
    )
    arrived = lax.all_to_all(outgoing, axes, split_axis=0, concat_axis=0, tiled=True)

    partial, late = pl.pallas_call(
        analyse_kernel,
        out_shape=(
            jax.ShapeDtypeStruct((2, degrees), F32),
            pltpu.VMEM((lat_band - first, degrees), F32),
        ),
        in_specs=[VMEM, ANY, ANY, VMEM],
        out_specs=(VMEM, VMEM),
        scratch_shapes=[
            pltpu.VMEM((2, lat_band, LANES), F32),
            pltpu.VMEM((groups, LANES), F32),
            pltpu.VMEM((2, 8, degrees), F32),
            pltpu.SemaphoreType.DMA,
            pltpu.SemaphoreType.DMA((groups - first // LANES,)),
        ],
        compiler_params=pltpu.CompilerParams(vmem_limit_bytes=12 * MIB),
        name="analyse",
    )(arrived, in_hbm(quad_weights.reshape(groups, LANES)), legendre, early)

    shares = [partial]
    for step in range(1, bands):
        moves = [
            (b * order_count + o, (b ^ step) * order_count + o)
            for b in range(bands)
            for o in range(order_count)
        ]
        shares.append(lax.ppermute(partial, axes, moves))
    while len(shares) > 4:
        shares = [shares[i] + shares[i + 1] for i in range(0, len(shares), 2)]

    coefficients, reply = pl.pallas_call(
        synthesise_kernel,
        out_shape=(
            jax.ShapeDtypeStruct((2, degrees), F32),
            jax.ShapeDtypeStruct((devices, 1, 2 * LANES), F32),
        ),
        in_specs=[VMEM] * 8,
        out_specs=(VMEM, VMEM),
        scratch_shapes=[
            pltpu.VMEM((2, 8, degrees), F32),
            pltpu.VMEM((LANES, LANES), F32),
        ],
        compiler_params=pltpu.CompilerParams(vmem_limit_bytes=12 * MIB),
        name="synthesise",
    )(*shares, love_code.reshape(1, degrees), arrived, early, late)
    answer = lax.all_to_all(reply, axes, split_axis=0, concat_axis=0, tiled=True)

    uplift = pl.pallas_call(
        functools.partial(return_kernel, bands),
        out_shape=jax.ShapeDtypeStruct((tiles, LANES), F32),
        in_specs=[VMEM] * 3,
        out_specs=VMEM,
        scratch_shapes=[pltpu.VMEM((2 * orders, tiles), F32)],
        compiler_params=pltpu.CompilerParams(vmem_limit_bytes=8 * MIB),
        name="give_back",
    )(answer, rot, basis)
    return uplift.reshape(tiles * LANES), coefficients.reshape(1, 2, degrees)


def solution(mesh):
    bands, order_count = mesh.shape["band"], mesh.shape["order"]
    assert bands & (bands - 1) == 0 and bands >= 4
    return jax.shard_map(
        functools.partial(on_device, bands, order_count),
        mesh=mesh,
        in_specs=(
            P(("band", "order")),
            P(("band", "order"), None, None),
            P(("band", "order"), None),
            P(("band", "order")),
            P(("band", "order")),
            P(),
            P("band"),
            P("order", "band", None),
            P(),
        ),
        out_specs=(P(("band", "order")), P("order", None, None)),
        check_vma=False,
    )
```

```python
import functools
import math

import jax
import jax.numpy as jnp
from jax import lax
from jax.experimental import pallas as pl
from jax.experimental.pallas import tpu as pltpu
from jax.sharding import PartitionSpec as P

NLON = 8192
LANES = 128
BLOCKS = NLON // LANES
SIZES = (64, 40, 24)
F32 = jnp.float32
BF16 = jnp.bfloat16
MIB = 1 << 20


def split(x, parts):
    out = []
    for _ in range(parts):
        piece = x.astype(BF16)
        out.append(piece)
        x = x - piece.astype(F32)
    return out


def chunks(tiles):
    sizes = SIZES
    starts = [sum(sizes[:i]) for i in range(len(sizes))]
    assert sum(sizes) == tiles
    return list(zip(starts, sizes))


def trig(phase, period):
    angle = phase.astype(F32) * (2.0 * math.pi / period)
    return jnp.cos(angle), jnp.sin(angle)


def project_kernel(
    lat_dev,
    window_hbm,
    thickness_hbm,
    dest_hbm,
    row_hbm,
    col_hbm,
    quad_hbm,
    weights,
    basis,
    rot,
    turned,
    sums_out,
    latitude,
    held,
    window,
    thickness,
    dest,
    row,
    col,
    quad,
    sems,
):
    tiles = held.shape[0]
    orders = window.shape[0]
    cuts = chunks(tiles)
    copies = [
        pltpu.make_async_copy(
            weights.at[pl.ds(first, count)], held.at[pl.ds(first, count)], sems.at[c]
        )
        for c, (first, count) in enumerate(cuts)
    ]
    small = [
        pltpu.make_async_copy(src, dst, sems.at[len(cuts) + i])
        for i, (src, dst) in enumerate(
            (
                (window_hbm, window),
                (col_hbm, col),
                (thickness_hbm, thickness),
                (dest_hbm, dest),
                (row_hbm, row),
                (quad_hbm, quad),
            )
        )
    ]
    for copy in small + copies:
        copy.start()
    for copy in small:
        copy.wait()
    weight = quad[...]
    blank = jnp.zeros((LANES - 2 * weight.shape[0], LANES), F32)
    turned[...] = jnp.transpose(jnp.concatenate([weight, weight, blank], axis=0))
    sub = lax.broadcasted_iota(jnp.int32, (orders, LANES), 0)
    lane = lax.broadcasted_iota(jnp.int32, (orders, LANES), 1)
    order = jnp.zeros((orders, LANES), jnp.int32)
    for m in range(orders):
        order = jnp.where(sub == m, window[m], order)
    cos_in, sin_in = trig((order * lane) & (NLON - 1), NLON)
    cos_block, sin_block = trig((order * col[...]) & (BLOCKS - 1), BLOCKS)
    rot[:orders] = cos_block
    rot[orders:] = sin_block
    inner = jnp.concatenate([cos_in, sin_in], axis=0)
    high, low = split(inner, 2)
    left = jnp.concatenate([high, low], axis=0)
    left = jnp.concatenate([left, left], axis=1)
    wide_lane = lax.broadcasted_iota(jnp.int32, (2 * orders, LANES), 1)
    sums = jnp.zeros((2 * orders, tiles), F32)
    for c, (first, count) in enumerate(cuts):
        copies[c].wait()
        pieces = []
        for i in range(count):
            high, low = split(held[first + i], 2)
            pieces.append(jnp.concatenate([high, low], axis=0))
        product = jnp.dot(left, jnp.concatenate(pieces, axis=1), preferred_element_type=F32)
        product = product[: 2 * orders] + product[2 * orders :]
        for i in range(count):
            t = first + i
            mine = product[:, i * LANES : (i + 1) * LANES]
            basis[t] = mine
            total = jnp.sum(mine * thickness[t : t + 1, :], axis=1, keepdims=True)
            sums = jnp.where(wide_lane == t, total, sums)
    sums_out[...] = sums
    latitude[...] = dest[...] * lat_dev + row[...]


def address_kernel(bands, order_count, lat_band, sums, rot, latitude, outgoing):
    orders = rot.shape[0] // 2
    cos_block, sin_block = rot[:orders], rot[orders:]
    by_cos, by_sin = sums[:orders], sums[orders:]
    scale = NLON**-0.5
    cos_part = (by_cos * cos_block - by_sin * sin_block) * scale
    sin_part = (by_cos * sin_block + by_sin * cos_block) * scale
    for b in range(bands):
        place = (latitude[...] - b * lat_band).astype(F32)
        for o in range(order_count):
            d = b * order_count + o
            outgoing[d, :, 0:LANES] = cos_part[o : o + 1]
            outgoing[d, :, LANES : 2 * LANES] = sin_part[o : o + 1]
            outgoing[d, :, 2 * LANES : 3 * LANES] = place


def places(arrived, s):
    latitude = arrived[s, :, 2 * LANES : 3 * LANES].astype(jnp.int32)
    return latitude >> 7, latitude & (LANES - 1)


def selector(arrived, s):
    sub = lax.broadcasted_iota(jnp.int32, (LANES, LANES), 0)
    _, low = places(arrived, s)
    return jnp.where(sub == low, 1.0, 0.0).astype(BF16)


def analyse_kernel(arrived, turned, legendre, partial, spread):
    devices = arrived.shape[0]
    groups = legendre.shape[0] // LANES
    rows = 2 * groups
    sub = lax.broadcasted_iota(jnp.int32, (rows, LANES), 0)
    group = jnp.where(sub >= groups, sub - groups, sub)
    select, value = [], []
    for s in range(devices):
        high, _ = places(arrived, s)
        both = jnp.where(
            sub < groups, arrived[s, :, 0:LANES], arrived[s, :, LANES : 2 * LANES]
        )
        value.append(jnp.where(group == high, both, 0.0))
        select.append(selector(arrived, s))
    select = jnp.concatenate(select, axis=1)
    value = jnp.concatenate(value, axis=1)
    spectra = jnp.zeros((LANES, rows), F32)
    for piece in reversed(split(value, 3)):
        spectra = spectra + lax.dot_general(
            select, piece, (((1,), (1,)), ((), ())), preferred_element_type=F32
        )
    spectra = spectra * turned[:, :rows]
    for e in range(2):
        for h in range(groups):
            k = e * groups + h
            spread[e, h * LANES : (h + 1) * LANES, :] = jnp.broadcast_to(
                spectra[:, k : k + 1], (LANES, LANES)
            )
    wide = 8
    degrees = legendre.shape[1]
    for start in range(0, degrees, wide * LANES):

        def body(h, sums):
            sums = list(sums)
            for j in range(LANES // 8):
                at = pl.ds(pl.multiple_of(h * LANES, LANES) + j * 8, 8)
                first, second = spread[0, at, :], spread[1, at, :]
                for k in range(wide):
                    p = legendre[at, start + k * LANES : start + (k + 1) * LANES]
                    sums[2 * k] = sums[2 * k] + p * first
                    sums[2 * k + 1] = sums[2 * k + 1] + p * second
            return tuple(sums)

        sums = lax.fori_loop(0, groups, body, (jnp.zeros((8, LANES), F32),) * (2 * wide))
        for k in range(wide):
            for e in range(2):
                partial[e : e + 1, start + k * LANES : start + (k + 1) * LANES] = jnp.sum(
                    sums[2 * k + e], axis=0, keepdims=True
                )


def synthesise_kernel(
    share_0, share_1, share_2, share_3, love, arrived, legendre, coefficients, reply, spread, fields
):
    devices = arrived.shape[0]
    lat_band, degrees = legendre.shape
    groups = lat_band // LANES
    rows = 2 * groups
    total = (share_0[...] + share_1[...]) + (share_2[...] + share_3[...])
    scaled = total * (love[...].astype(F32) / 1000.0)
    coefficients[...] = scaled
    for e in range(2):
        spread[e] = jnp.broadcast_to(scaled[e : e + 1], (8, degrees))
    lane = lax.broadcasted_iota(jnp.int32, (8, LANES), 1)
    fields[...] = jnp.zeros_like(fields)

    def body(h, carry):
        for half in range(2):
            sums = [jnp.zeros((8, LANES), F32)] * 16
            for k in range(degrees // LANES):
                cut = slice(k * LANES, (k + 1) * LANES)
                first, second = spread[0, :, cut], spread[1, :, cut]
                for i in range(8):
                    at = pl.ds(h * LANES + (half * 8 + i) * 8, 8)
                    p = legendre[at, cut]
                    sums[2 * i] = sums[2 * i] + p * first
                    sums[2 * i + 1] = sums[2 * i + 1] + p * second
            for i in range(8):
                g = half * 8 + i
                first = jnp.sum(sums[2 * i], axis=1, keepdims=True)
                second = jnp.sum(sums[2 * i + 1], axis=1, keepdims=True)
                old = fields[g * 8 : (g + 1) * 8, :]
                old = jnp.where(lane == h, first, old)
                fields[g * 8 : (g + 1) * 8, :] = jnp.where(lane == h + groups, second, old)
        return carry

    for h in range(groups):
        body(h, 0)
    turned = jnp.transpose(fields[...])[:rows]
    select = jnp.concatenate([selector(arrived, s) for s in range(devices)], axis=1)
    found = jnp.zeros((rows, devices * LANES), F32)
    for piece in reversed(split(turned, 3)):
        found = found + jnp.dot(piece, select, preferred_element_type=F32)
    sub = lax.broadcasted_iota(jnp.int32, (rows, LANES), 0)
    group = jnp.where(sub >= groups, sub - groups, sub)
    for s in range(devices):
        high, _ = places(arrived, s)
        here = jnp.where(group == high, found[:, s * LANES : (s + 1) * LANES], 0.0)
        reply[s, :, 0:LANES] = jnp.sum(here[:groups], axis=0, keepdims=True)
        reply[s, :, LANES : 2 * LANES] = jnp.sum(here[groups:], axis=0, keepdims=True)


def return_kernel(bands, answer, rot, basis, uplift, at_tile):
    tiles = basis.shape[0]
    orders = rot.shape[0] // 2
    order_count = answer.shape[0] // bands
    for e in range(2):
        for o in range(order_count):
            got = answer[o, :, e * LANES : (e + 1) * LANES]
            for b in range(1, bands):
                got = got + answer[b * order_count + o, :, e * LANES : (e + 1) * LANES]
            at_tile[e * orders + o : e * orders + o + 1, :] = got
    by_cos, by_sin = at_tile[:orders], at_tile[orders:]
    cos_block, sin_block = rot[:orders], rot[orders:]
    scale = (2 * orders) ** -0.5
    turned = jnp.concatenate(
        [
            (by_cos * cos_block + by_sin * sin_block) * scale,
            (by_sin * cos_block - by_cos * sin_block) * scale,
        ],
        axis=0,
    )
    for t in range(tiles):
        uplift[t : t + 1, :] = jnp.sum(basis[t] * turned[:, t : t + 1], axis=0, keepdims=True)


def in_hbm(x):
    return pltpu.with_memory_space_constraint(x, pltpu.HBM)


VMEM = pl.BlockSpec(memory_space=pltpu.VMEM)
ANY = pl.BlockSpec(memory_space=pl.ANY)


def on_device(
    bands,
    order_count,
    thickness,
    tile_weights,
    tile_dest,
    tile_row,
    tile_col,
    window,
    quad_weights,
    legendre,
    love_code,
):
    devices = bands * order_count
    axes = ("band", "order")
    tiles = tile_weights.shape[0]
    lat_band = quad_weights.shape[0]
    orders = window.shape[0]
    degrees = legendre.shape[2]
    assert tiles == LANES and legendre.shape[0] == 1 and orders == order_count
    assert lat_band % LANES == 0 and degrees % (8 * LANES) == 0
    legendre = legendre.reshape(lat_band, degrees)
    groups = lat_band // LANES

    basis, rot, turned, sums, latitude = pl.pallas_call(
        functools.partial(project_kernel, lat_band // order_count),
        out_shape=(
            jax.ShapeDtypeStruct((tiles, 2 * orders, LANES), F32),
            jax.ShapeDtypeStruct((2 * orders, tiles), F32),
            jax.ShapeDtypeStruct((LANES, LANES), F32),
            jax.ShapeDtypeStruct((2 * orders, tiles), F32),
            jax.ShapeDtypeStruct((1, tiles), jnp.int32),
        ),
        in_specs=[ANY] * 7,
        out_specs=(VMEM,) * 5,
        scratch_shapes=[
            pltpu.VMEM((tiles, LANES, LANES), F32),
            pltpu.SMEM((orders,), jnp.int32),
            pltpu.VMEM((tiles, LANES), F32),
            pltpu.VMEM((1, tiles), jnp.int32),
            pltpu.VMEM((1, tiles), jnp.int32),
            pltpu.VMEM((1, tiles), jnp.int32),
            pltpu.VMEM((groups, LANES), F32),
            pltpu.SemaphoreType.DMA((len(chunks(tiles)) + 6,)),
        ],
        compiler_params=pltpu.CompilerParams(vmem_limit_bytes=20 * MIB),
        name="project",
    )(
        in_hbm(window),
        in_hbm(thickness.reshape(tiles, LANES)),
        in_hbm(tile_dest.reshape(1, tiles)),
        in_hbm(tile_row.reshape(1, tiles)),
        in_hbm(tile_col.reshape(1, tiles)),
        in_hbm(quad_weights.reshape(groups, LANES)),
        in_hbm(tile_weights),
    )
    outgoing = pl.pallas_call(
        functools.partial(address_kernel, bands, order_count, lat_band),
        out_shape=jax.ShapeDtypeStruct((devices, 1, 3 * LANES), F32),
        in_specs=[VMEM] * 3,
        out_specs=VMEM,
        compiler_params=pltpu.CompilerParams(vmem_limit_bytes=4 * MIB),
        cost_estimate=pl.CostEstimate(
            flops=10**12, transcendentals=0, bytes_accessed=MIB
        ),
        name="address",
    )(sums, rot, latitude)

    arrived = lax.all_to_all(outgoing, axes, split_axis=0, concat_axis=0, tiled=True)

    partial = pl.pallas_call(
        analyse_kernel,
        out_shape=jax.ShapeDtypeStruct((2, degrees), F32),
        in_specs=[VMEM] * 3,
        out_specs=VMEM,
        scratch_shapes=[
            pltpu.VMEM((2, lat_band, LANES), F32),
        ],
        compiler_params=pltpu.CompilerParams(vmem_limit_bytes=12 * MIB),
        name="analyse",
    )(arrived, turned, legendre)

    shares = [partial]
    for step in range(1, bands):
        moves = [
            (b * order_count + o, (b ^ step) * order_count + o)
            for b in range(bands)
            for o in range(order_count)
        ]
        shares.append(lax.ppermute(partial, axes, moves))
    while len(shares) > 4:
        shares = [shares[i] + shares[i + 1] for i in range(0, len(shares), 2)]

    coefficients, reply = pl.pallas_call(
        synthesise_kernel,
        out_shape=(
            jax.ShapeDtypeStruct((2, degrees), F32),
            jax.ShapeDtypeStruct((devices, 1, 2 * LANES), F32),
        ),
        in_specs=[VMEM] * 7,
        out_specs=(VMEM, VMEM),
        scratch_shapes=[
            pltpu.VMEM((2, 8, degrees), F32),
            pltpu.VMEM((LANES, LANES), F32),
        ],
        compiler_params=pltpu.CompilerParams(vmem_limit_bytes=12 * MIB),
        name="synthesise",
    )(*shares, love_code.reshape(1, degrees), arrived, legendre)
    answer = lax.all_to_all(reply, axes, split_axis=0, concat_axis=0, tiled=True)

    uplift = pl.pallas_call(
        functools.partial(return_kernel, bands),
        out_shape=jax.ShapeDtypeStruct((tiles, LANES), F32),
        in_specs=[VMEM] * 3,
        out_specs=VMEM,
        scratch_shapes=[pltpu.VMEM((2 * orders, tiles), F32)],
        compiler_params=pltpu.CompilerParams(vmem_limit_bytes=8 * MIB),
        name="give_back",
    )(answer, rot, basis)
    return uplift.reshape(tiles * LANES), coefficients.reshape(1, 2, degrees)


def solution(mesh):
    bands, order_count = mesh.shape["band"], mesh.shape["order"]
    assert bands & (bands - 1) == 0 and bands >= 4
    return jax.shard_map(
        functools.partial(on_device, bands, order_count),
        mesh=mesh,
        in_specs=(
            P(("band", "order")),
            P(("band", "order"), None, None),
            P(("band", "order"), None),
            P(("band", "order")),
            P(("band", "order")),
            P(),
            P("band"),
            P("order", "band", None),
            P(),
        ),
        out_specs=(P(("band", "order")), P("order", None, None)),
        check_vma=False,
    )
```

```python
import functools
import math

import jax
import jax.numpy as jnp
from jax import lax
from jax.experimental import pallas as pl
from jax.experimental.pallas import tpu as pltpu
from jax.sharding import PartitionSpec as P

NLON = 8192
LANES = 128
BLOCKS = NLON // LANES
SIZES = (32, 32, 32, 32)
F32 = jnp.float32
BF16 = jnp.bfloat16
MIB = 1 << 20


def split(x, parts):
    out = []
    for _ in range(parts):
        piece = x.astype(BF16)
        out.append(piece)
        x = x - piece.astype(F32)
    return out


def chunks(tiles):
    sizes = SIZES
    starts = [sum(sizes[:i]) for i in range(len(sizes))]
    assert sum(sizes) == tiles
    return list(zip(starts, sizes))


def stacked(x):
    return jnp.concatenate([p.astype(F32) for p in split(x, 3)], axis=0).astype(BF16)


def trig(phase, period):
    angle = phase.astype(F32) * (2.0 * math.pi / period)
    return jnp.cos(angle), jnp.sin(angle)


def project_kernel(
    lat_dev,
    window_hbm,
    thickness_hbm,
    dest_hbm,
    row_hbm,
    col_hbm,
    quad_hbm,
    weights,
    basis,
    rot,
    turned,
    sums_out,
    latitude,
    held,
    window,
    thickness,
    dest,
    row,
    col,
    quad,
    sems,
):
    tiles = held.shape[0]
    orders = window.shape[0]
    cuts = chunks(tiles)
    copies = [
        pltpu.make_async_copy(
            weights.at[pl.ds(first, count)], held.at[pl.ds(first, count)], sems.at[c]
        )
        for c, (first, count) in enumerate(cuts)
    ]
    small = [
        pltpu.make_async_copy(src, dst, sems.at[len(cuts) + i])
        for i, (src, dst) in enumerate(
            (
                (window_hbm, window),
                (col_hbm, col),
                (thickness_hbm, thickness),
                (dest_hbm, dest),
                (row_hbm, row),
                (quad_hbm, quad),
            )
        )
    ]
    for copy in small + copies:
        copy.start()
    for copy in small:
        copy.wait()
    weight = quad[...]
    blank = jnp.zeros((LANES - 2 * weight.shape[0], LANES), F32)
    turned[...] = jnp.transpose(jnp.concatenate([weight, weight, blank], axis=0))
    sub = lax.broadcasted_iota(jnp.int32, (orders, LANES), 0)
    lane = lax.broadcasted_iota(jnp.int32, (orders, LANES), 1)
    order = jnp.zeros((orders, LANES), jnp.int32)
    for m in range(orders):
        order = jnp.where(sub == m, window[m], order)
    cos_in, sin_in = trig((order * lane) & (NLON - 1), NLON)
    cos_block, sin_block = trig((order * col[...]) & (BLOCKS - 1), BLOCKS)
    rot[:orders] = cos_block
    rot[orders:] = sin_block
    inner = jnp.concatenate([cos_in, sin_in], axis=0)
    high, low = split(inner, 2)
    left = jnp.concatenate([high, low], axis=0)
    left = jnp.concatenate([left, left], axis=1)
    wide_lane = lax.broadcasted_iota(jnp.int32, (2 * orders, LANES), 1)
    sums = jnp.zeros((2 * orders, tiles), F32)
    for c, (first, count) in enumerate(cuts):
        copies[c].wait()
        pieces = []
        for i in range(count):
            high, low = split(held[first + i], 2)
            pieces.append(jnp.concatenate([high, low], axis=0))
        product = jnp.dot(left, jnp.concatenate(pieces, axis=1), preferred_element_type=F32)
        product = product[: 2 * orders] + product[2 * orders :]
        for i in range(count):
            t = first + i
            mine = product[:, i * LANES : (i + 1) * LANES]
            basis[t] = mine
            total = jnp.sum(mine * thickness[t : t + 1, :], axis=1, keepdims=True)
            sums = jnp.where(wide_lane == t, total, sums)
    sums_out[...] = sums
    latitude[...] = dest[...] * lat_dev + row[...]


def address_kernel(bands, order_count, lat_band, sums, rot, latitude, outgoing):
    orders = rot.shape[0] // 2
    cos_block, sin_block = rot[:orders], rot[orders:]
    by_cos, by_sin = sums[:orders], sums[orders:]
    scale = NLON**-0.5
    cos_part = (by_cos * cos_block - by_sin * sin_block) * scale
    sin_part = (by_cos * sin_block + by_sin * cos_block) * scale
    for b in range(bands):
        place = (latitude[...] - b * lat_band).astype(F32)
        for o in range(order_count):
            d = b * order_count + o
            outgoing[d, :, 0:LANES] = cos_part[o : o + 1]
            outgoing[d, :, LANES : 2 * LANES] = sin_part[o : o + 1]
            outgoing[d, :, 2 * LANES : 3 * LANES] = place


def places(arrived, s):
    latitude = arrived[s, :, 2 * LANES : 3 * LANES].astype(jnp.int32)
    return latitude >> 7, latitude & (LANES - 1)


def selector(arrived, s):
    sub = lax.broadcasted_iota(jnp.int32, (LANES, LANES), 0)
    _, low = places(arrived, s)
    return jnp.where(sub == low, 1.0, 0.0).astype(BF16)


def analyse_kernel(arrived, turned, legendre, partial, select, spread):
    devices = arrived.shape[0]
    groups = legendre.shape[0] // LANES
    rows = 2 * groups
    sub = lax.broadcasted_iota(jnp.int32, (rows, LANES), 0)
    group = jnp.where(sub >= groups, sub - groups, sub)
    value = []
    for s in range(devices):
        high, _ = places(arrived, s)
        both = jnp.where(
            sub < groups, arrived[s, :, 0:LANES], arrived[s, :, LANES : 2 * LANES]
        )
        value.append(jnp.where(group == high, both, 0.0))
        select[:, s * LANES : (s + 1) * LANES] = selector(arrived, s)
    value = jnp.concatenate(value, axis=1)
    spectra = lax.dot_general(
        select[...], stacked(value), (((1,), (1,)), ((), ())), preferred_element_type=F32
    )
    spectra = (spectra[:, 2 * rows :] + spectra[:, rows : 2 * rows]) + spectra[:, :rows]
    spectra = spectra * turned[:, :rows]
    for e in range(2):
        for h in range(groups):
            k = e * groups + h
            spread[e, h * LANES : (h + 1) * LANES, :] = jnp.broadcast_to(
                spectra[:, k : k + 1], (LANES, LANES)
            )
    wide = 8
    degrees = legendre.shape[1]
    for start in range(0, degrees, wide * LANES):

        def body(h, sums):
            sums = list(sums)
            for j in range(LANES // 8):
                at = pl.ds(pl.multiple_of(h * LANES, LANES) + j * 8, 8)
                first, second = spread[0, at, :], spread[1, at, :]
                for k in range(wide):
                    p = legendre[at, start + k * LANES : start + (k + 1) * LANES]
                    sums[2 * k] = sums[2 * k] + p * first
                    sums[2 * k + 1] = sums[2 * k + 1] + p * second
            return tuple(sums)

        sums = lax.fori_loop(0, groups, body, (jnp.zeros((8, LANES), F32),) * (2 * wide))
        for k in range(wide):
            for e in range(2):
                partial[e : e + 1, start + k * LANES : start + (k + 1) * LANES] = jnp.sum(
                    sums[2 * k + e], axis=0, keepdims=True
                )


def synthesise_kernel(
    share_0, share_1, share_2, share_3, love, arrived, select, legendre, coefficients, reply, spread, fields
):
    devices = arrived.shape[0]
    lat_band, degrees = legendre.shape
    groups = lat_band // LANES
    rows = 2 * groups
    total = (share_0[...] + share_1[...]) + (share_2[...] + share_3[...])
    scaled = total * (love[...].astype(F32) / 1000.0)
    coefficients[...] = scaled
    for e in range(2):
        spread[e] = jnp.broadcast_to(scaled[e : e + 1], (8, degrees))
    lane = lax.broadcasted_iota(jnp.int32, (8, LANES), 1)
    fields[...] = jnp.zeros_like(fields)

    def body(h, carry):
        for half in range(2):
            sums = [jnp.zeros((8, LANES), F32)] * 16
            for k in range(degrees // LANES):
                cut = slice(k * LANES, (k + 1) * LANES)
                first, second = spread[0, :, cut], spread[1, :, cut]
                for i in range(8):
                    at = pl.ds(h * LANES + (half * 8 + i) * 8, 8)
                    p = legendre[at, cut]
                    sums[2 * i] = sums[2 * i] + p * first
                    sums[2 * i + 1] = sums[2 * i + 1] + p * second
            for i in range(8):
                g = half * 8 + i
                first = jnp.sum(sums[2 * i], axis=1, keepdims=True)
                second = jnp.sum(sums[2 * i + 1], axis=1, keepdims=True)
                old = fields[g * 8 : (g + 1) * 8, :]
                old = jnp.where(lane == h, first, old)
                fields[g * 8 : (g + 1) * 8, :] = jnp.where(lane == h + groups, second, old)
        return carry

    for h in range(groups):
        body(h, 0)
    turned = jnp.transpose(fields[...])[:rows]
    found = jnp.dot(stacked(turned), select[...], preferred_element_type=F32)
    found = (found[2 * rows :] + found[rows : 2 * rows]) + found[:rows]
    sub = lax.broadcasted_iota(jnp.int32, (rows, LANES), 0)
    group = jnp.where(sub >= groups, sub - groups, sub)
    for s in range(devices):
        high, _ = places(arrived, s)
        here = jnp.where(group == high, found[:, s * LANES : (s + 1) * LANES], 0.0)
        reply[s, :, 0:LANES] = jnp.sum(here[:groups], axis=0, keepdims=True)
        reply[s, :, LANES : 2 * LANES] = jnp.sum(here[groups:], axis=0, keepdims=True)


def return_kernel(bands, answer, rot, basis, uplift, at_tile):
    tiles = basis.shape[0]
    orders = rot.shape[0] // 2
    order_count = answer.shape[0] // bands
    for e in range(2):
        for o in range(order_count):
            got = answer[o, :, e * LANES : (e + 1) * LANES]
            for b in range(1, bands):
                got = got + answer[b * order_count + o, :, e * LANES : (e + 1) * LANES]
            at_tile[e * orders + o : e * orders + o + 1, :] = got
    by_cos, by_sin = at_tile[:orders], at_tile[orders:]
    cos_block, sin_block = rot[:orders], rot[orders:]
    scale = (2 * orders) ** -0.5
    turned = jnp.concatenate(
        [
            (by_cos * cos_block + by_sin * sin_block) * scale,
            (by_sin * cos_block - by_cos * sin_block) * scale,
        ],
        axis=0,
    )
    for t in range(tiles):
        uplift[t : t + 1, :] = jnp.sum(basis[t] * turned[:, t : t + 1], axis=0, keepdims=True)


def in_hbm(x):
    return pltpu.with_memory_space_constraint(x, pltpu.HBM)


VMEM = pl.BlockSpec(memory_space=pltpu.VMEM)
ANY = pl.BlockSpec(memory_space=pl.ANY)


def on_device(
    bands,
    order_count,
    thickness,
    tile_weights,
    tile_dest,
    tile_row,
    tile_col,
    window,
    quad_weights,
    legendre,
    love_code,
):
    devices = bands * order_count
    axes = ("band", "order")
    tiles = tile_weights.shape[0]
    lat_band = quad_weights.shape[0]
    orders = window.shape[0]
    degrees = legendre.shape[2]
    assert tiles == LANES and legendre.shape[0] == 1 and orders == order_count
    assert lat_band % LANES == 0 and degrees % (8 * LANES) == 0
    legendre = legendre.reshape(lat_band, degrees)
    groups = lat_band // LANES

    basis, rot, turned, sums, latitude = pl.pallas_call(
        functools.partial(project_kernel, lat_band // order_count),
        out_shape=(
            jax.ShapeDtypeStruct((tiles, 2 * orders, LANES), F32),
            jax.ShapeDtypeStruct((2 * orders, tiles), F32),
            jax.ShapeDtypeStruct((LANES, LANES), F32),
            jax.ShapeDtypeStruct((2 * orders, tiles), F32),
            jax.ShapeDtypeStruct((1, tiles), jnp.int32),
        ),
        in_specs=[ANY] * 7,
        out_specs=(VMEM,) * 5,
        scratch_shapes=[
            pltpu.VMEM((tiles, LANES, LANES), F32),
            pltpu.SMEM((orders,), jnp.int32),
            pltpu.VMEM((tiles, LANES), F32),
            pltpu.VMEM((1, tiles), jnp.int32),
            pltpu.VMEM((1, tiles), jnp.int32),
            pltpu.VMEM((1, tiles), jnp.int32),
            pltpu.VMEM((groups, LANES), F32),
            pltpu.SemaphoreType.DMA((len(chunks(tiles)) + 6,)),
        ],
        compiler_params=pltpu.CompilerParams(vmem_limit_bytes=20 * MIB),
        name="project",
    )(
        in_hbm(window),
        in_hbm(thickness.reshape(tiles, LANES)),
        in_hbm(tile_dest.reshape(1, tiles)),
        in_hbm(tile_row.reshape(1, tiles)),
        in_hbm(tile_col.reshape(1, tiles)),
        in_hbm(quad_weights.reshape(groups, LANES)),
        in_hbm(tile_weights),
    )
    outgoing = pl.pallas_call(
        functools.partial(address_kernel, bands, order_count, lat_band),
        out_shape=jax.ShapeDtypeStruct((devices, 1, 3 * LANES), F32),
        in_specs=[VMEM] * 3,
        out_specs=VMEM,
        compiler_params=pltpu.CompilerParams(vmem_limit_bytes=4 * MIB),
        cost_estimate=pl.CostEstimate(
            flops=10**12, transcendentals=0, bytes_accessed=MIB
        ),
        name="address",
    )(sums, rot, latitude)

    arrived = lax.all_to_all(outgoing, axes, split_axis=0, concat_axis=0, tiled=True)

    partial, select = pl.pallas_call(
        analyse_kernel,
        out_shape=(
            jax.ShapeDtypeStruct((2, degrees), F32),
            jax.ShapeDtypeStruct((LANES, devices * LANES), BF16),
        ),
        in_specs=[VMEM] * 3,
        out_specs=(VMEM, VMEM),
        scratch_shapes=[
            pltpu.VMEM((2, lat_band, LANES), F32),
        ],
        compiler_params=pltpu.CompilerParams(vmem_limit_bytes=12 * MIB),
        name="analyse",
    )(arrived, turned, legendre)

    shares = [partial]
    for step in range(1, bands):
        moves = [
            (b * order_count + o, (b ^ step) * order_count + o)
            for b in range(bands)
            for o in range(order_count)
        ]
        shares.append(lax.ppermute(partial, axes, moves))
    while len(shares) > 4:
        shares = [shares[i] + shares[i + 1] for i in range(0, len(shares), 2)]

    coefficients, reply = pl.pallas_call(
        synthesise_kernel,
        out_shape=(
            jax.ShapeDtypeStruct((2, degrees), F32),
            jax.ShapeDtypeStruct((devices, 1, 2 * LANES), F32),
        ),
        in_specs=[VMEM] * 8,
        out_specs=(VMEM, VMEM),
        scratch_shapes=[
            pltpu.VMEM((2, 8, degrees), F32),
            pltpu.VMEM((LANES, LANES), F32),
        ],
        compiler_params=pltpu.CompilerParams(vmem_limit_bytes=12 * MIB),
        name="synthesise",
    )(*shares, love_code.reshape(1, degrees), arrived, select, legendre)
    answer = lax.all_to_all(reply, axes, split_axis=0, concat_axis=0, tiled=True)

    uplift = pl.pallas_call(
        functools.partial(return_kernel, bands),
        out_shape=jax.ShapeDtypeStruct((tiles, LANES), F32),
        in_specs=[VMEM] * 3,
        out_specs=VMEM,
        scratch_shapes=[pltpu.VMEM((2 * orders, tiles), F32)],
        compiler_params=pltpu.CompilerParams(vmem_limit_bytes=8 * MIB),
        name="give_back",
    )(answer, rot, basis)
    return uplift.reshape(tiles * LANES), coefficients.reshape(1, 2, degrees)


def solution(mesh):
    bands, order_count = mesh.shape["band"], mesh.shape["order"]
    assert bands & (bands - 1) == 0 and bands >= 4
    return jax.shard_map(
        functools.partial(on_device, bands, order_count),
        mesh=mesh,
        in_specs=(
            P(("band", "order")),
            P(("band", "order"), None, None),
            P(("band", "order"), None),
            P(("band", "order")),
            P(("band", "order")),
            P(),
            P("band"),
            P("order", "band", None),
            P(),
        ),
        out_specs=(P(("band", "order")), P("order", None, None)),
        check_vma=False,
    )
```
